32 devices in a mesh: seq: 16 (over z, y, core), head: 2 (over x).
Axes of the slice: x: 2, y: 2, z: 4, core: 2. Of those that a mesh axis runs over, the one named last changes fastest.
Arguments:
- query_rows: bfloat16 [24576, 2048], P('seq', 'head'), may hold values from -8 to 8
- key_rows: bfloat16 [24576, 2048], P('seq', 'head'), may hold values from -8 to 8
- value_rows: bfloat16 [24576, 2048], P('seq', 'head'), may hold values from -6 to 6
- head_phase: int32 [16], P('head'), may hold values from 0 to 15, each once
- out_weight: bfloat16 [2048, 2048], P('head'), may hold values from -0.125 to 0.125
Outputs:
- projected: bfloat16 [24576, 2048], P(('seq', 'head'))
The draws below stay inside these ranges and needn't reach their ends.
Inputs may be any that keep to these rules, and one draw needn't show every extreme that they name: `head_phase`: the 16 heads have distinct phases.
All inputs are finite; a program needn't handle non-finite values.
Results may differ from the reference program's by a relative error of at most 0.006.
Values may be sent and summed in bfloat16 or wider, within the bound.
No kernel may reach another device: no remote copies, remote signals or barrier semaphores. Data moves between devices by JAX's collectives and lax.ppermute only.
A program may use at most 256 MiB of HBM per device.

```python
import math
import jax
import jax.numpy as jnp
from jax import lax

D = 2048
H = 16
HEAD_DIM = 128
TOK_DEV = 1536
HD = 2048
TOKENS = 24576
LEVELS = 4
N_HEAD = 2


def drawn(key, salt_value):
    full_width = H * HEAD_DIM
    base_key = jax.random.fold_in(key, salt_value)
    base_values = 2.0 * jax.random.normal(base_key, (TOKENS, full_width), jnp.float32)
    return jnp.clip(base_values, -8.0, 8.0).astype(jnp.bfloat16)


def draw_query_rows(key, part):
    return drawn(key, 1)


def draw_key_rows(key, part):
    return drawn(key, 2)


def levels(own_key, shape, shards, low, high):
    def one(position, parts):
        heights = jax.random.uniform(jax.random.fold_in(jax.random.fold_in(own_key, 6), position), (parts,), jnp.float32, low / len(shards), high / len(shards))
        return jnp.repeat(jnp.exp(heights), shape[position] // parts).reshape((-1,) + (1,) * (len(shape) - position - 1))

    loudness = one(*shards[0])
    for cut in shards[1:]:
        loudness = loudness * one(*cut)
    return loudness


def noise(key, shape, scale, bound, pieces=(), kind=jnp.bfloat16):
    loudness = levels(key, shape, pieces, -0.22, 0.18) if pieces else 1.0
    result = jax.random.normal(key, shape, jnp.float32) * scale * loudness
    return jnp.minimum(jnp.maximum(result, -bound), bound).astype(kind)


def setup_inputs(seed: int = 0) -> dict:
    keys = jax.random.split(jax.random.key(seed), 6)
    return {
        "query_rows": draw_query_rows(jax.random.fold_in(keys[5], 71), 0),
        "key_rows": draw_key_rows(jax.random.fold_in(keys[5], 71), 0),
        "value_rows": noise(keys[2], (TOKENS, HD), 1.0, 6.0, ((0, 16), (1, 2))),
        "head_phase": jax.random.permutation(keys[3], H).astype(jnp.int32),
        "out_weight": noise(keys[4], (HD, D), HD ** -0.5, 0.125, ((0, 2),)),
    }


def select_rows(block, offset, stride):
    row_count = block.shape[0] // stride
    shaped = block.reshape(row_count, stride, block.shape[1])
    return lax.dynamic_slice_in_dim(shaped, offset, 1, 1)[:, 0]

def place_rows(merged, fresh, offset, stride):
    row_count = merged.shape[0] // stride
    shaped = merged.reshape(row_count, stride, merged.shape[1])
    return lax.dynamic_update_slice_in_dim(shaped, fresh[:, None], offset, 1).reshape(merged.shape)

def segment_attention(segment_parts):
    queries, keys_in, values_in = segment_parts
    scores = jnp.einsum('qd,kd->qk', queries, keys_in) * (1.0 / math.sqrt(HEAD_DIM))
    row_peak = lax.optimization_barrier(jnp.max(scores, axis=1))
    weights = jnp.exp(scores - row_peak[:, None])
    row_total = lax.optimization_barrier(jnp.sum(weights, axis=1))
    rounded = lax.optimization_barrier(weights.astype(jnp.bfloat16)).astype(jnp.float32)
    row_mixed = jnp.einsum('qk,kd->qd', rounded, values_in)
    return (row_peak, row_total, row_mixed)

def reference(query_rows, key_rows, value_rows, head_phase, out_weight):
    tokens = query_rows.shape[0]
    attended = []
    for head_index in range(H):
        first_col = head_index * HEAD_DIM
        head_query = query_rows[:, first_col:first_col + HEAD_DIM].astype(jnp.float32)
        head_key = key_rows[:, first_col:first_col + HEAD_DIM].astype(jnp.float32)
        head_value = value_rows[:, first_col:first_col + HEAD_DIM].astype(jnp.float32)
        for level_index in range(LEVELS + 1):
            stride = 2 ** level_index
            offset = (head_phase[head_index] % stride).astype(jnp.int32)
            segments = tokens // (TOK_DEV * stride)
            picked = tuple((select_rows(source, offset, stride).reshape(segments, TOK_DEV, HEAD_DIM) for source in (head_query, head_key, head_value)))
            row_peak, row_total, row_mixed = lax.map(segment_attention, picked)
            row_peak = row_peak.reshape(-1)
            row_total = row_total.reshape(-1)
            row_mixed = row_mixed.reshape(-1, HEAD_DIM)
            if level_index == 0:
                peaks, totals, sums = (row_peak, row_total, row_mixed)
            else:
                old_peak = select_rows(peaks[:, None], offset, stride)[:, 0]
                old_total = select_rows(totals[:, None], offset, stride)[:, 0]
                old_sum = select_rows(sums, offset, stride)
                new_peak = jnp.maximum(old_peak, row_peak)
                keep_scale = jnp.exp(old_peak - new_peak)
                fresh_scale = jnp.exp(row_peak - new_peak)
                new_total = old_total * keep_scale + row_total * fresh_scale
                new_sum = old_sum * keep_scale[:, None] + row_mixed * fresh_scale[:, None]
                peaks = place_rows(peaks[:, None], new_peak[:, None], offset, stride)[:, 0]
                totals = place_rows(totals[:, None], new_total[:, None], offset, stride)[:, 0]
                sums = place_rows(sums, new_sum, offset, stride)
        attended.append((sums / totals[:, None]).astype(jnp.bfloat16))
    attended = jnp.concatenate(attended, axis=1)
    group_cols = H // N_HEAD * HEAD_DIM
    running = jnp.zeros((tokens, D), jnp.float32)
    for group_index in range(N_HEAD):
        low = group_index * group_cols
        term_part = jnp.dot(attended[:, low:low + group_cols], out_weight[low:low + group_cols], preferred_element_type=jnp.float32)
        running = running + lax.optimization_barrier(term_part.astype(jnp.bfloat16)).astype(jnp.float32)
    return running.astype(jnp.bfloat16)
```

```python
import functools
import math

import numpy as np
import jax
import jax.numpy as jnp
from jax import lax
from jax.experimental import pallas as pl
from jax.experimental.pallas import tpu as pltpu
from jax.sharding import PartitionSpec as P

ROW_TILE = 16
LOG2E = 1.4426950408889634
MASKED = -1.0e30


def bit_reverse(value, bits):
    result = 0
    for bit in range(bits):
        result |= ((value >> bit) & 1) << (bits - 1 - bit)
    return result


def slot_class(slot, levels):
    return levels - slot.bit_length()


def swapped(value, axis, bit):
    mask = 2**bit
    pairs = [(source, source ^ mask) for source in range(lax.axis_size(axis))]
    return lax.ppermute(value, axis, pairs)


def one_hot_order(size, stride, transposed):
    rows = lax.broadcasted_iota(jnp.int32, (size, size), 0)
    cols = lax.broadcasted_iota(jnp.int32, (size, size), 1)
    if transposed:
        rows, cols = cols, rows
    inner = size // stride
    match = (rows % inner) * stride + rows // inner == cols
    return jnp.where(match, 1.0, 0.0).astype(jnp.bfloat16)


def reorder_kernel(table, *refs, sources, groups, slots, cuts):
    source_refs = refs[:sources]
    out_refs = refs[sources:-1]
    scratch = refs[-1]
    size = source_refs[0].shape[0]
    order = one_hot_order(size, slots, False)
    for index in range(sources):
        moved = jnp.dot(order, source_refs[index][...], preferred_element_type=jnp.float32)
        scratch[index] = moved.astype(jnp.bfloat16).reshape(slots, ROW_TILE, moved.shape[1])
    for head in range(groups):
        for slot in range(slots):
            residue = table[head, slot]
            for index in range(sources):
                piece = scratch[index, residue, :, head * 128 : (head + 1) * 128]
                for out_ref, (low, high) in zip(out_refs, cuts):
                    if low <= slot < high:
                        out_ref[index, head, slot - low] = piece


def reorder(table, arrays, slots, cuts):
    rows, cols = arrays[0].shape
    groups = cols // 128
    size = slots * ROW_TILE
    blocks = rows // size
    inner = rows // slots
    sources = len(arrays)
    out_shape = [
        jax.ShapeDtypeStruct((sources, groups, high - low, inner, 128), jnp.bfloat16)
        for low, high in cuts
    ]
    total = sum(high - low for low, high in cuts)
    return pl.pallas_call(
        functools.partial(
            reorder_kernel, sources=sources, groups=groups, slots=slots, cuts=cuts
        ),
        out_shape=out_shape,
        grid_spec=pltpu.PrefetchScalarGridSpec(
            num_scalar_prefetch=1,
            grid=(blocks,),
            in_specs=[pl.BlockSpec((size, cols), lambda b, t: (b, 0))] * sources,
            out_specs=[
                pl.BlockSpec(
                    (sources, groups, high - low, ROW_TILE, 128), lambda b, t: (0, 0, 0, b, 0)
                )
                for low, high in cuts
            ],
            scratch_shapes=[pltpu.VMEM((sources, slots, ROW_TILE, cols), jnp.bfloat16)],
        ),
        compiler_params=pltpu.CompilerParams(vmem_limit_bytes=56 << 20),
        cost_estimate=pl.CostEstimate(
            flops=2 * sources * rows * size * cols,
            transcendentals=0,
            bytes_accessed=2 * sources * rows * cols + 2 * sources * groups * total * inner * 128,
        ),
        name="reorder",
    )(table, *arrays)


def attention_kernel(
    own_x, q_ref, *refs, parts, tiles, has_bias, has_state, state_rows, owners, score_scale
):
    refs = list(refs)
    kv_refs = [refs.pop(0) for _ in range(parts)]
    bias_ref = refs.pop(0) if has_bias else None
    state_in = [refs.pop(0) for _ in range(3)] if has_state else None
    mine_ref = refs.pop(0)
    theirs_ref = refs.pop(0)
    state_out = [refs.pop(0) for _ in range(3)] if state_rows else None
    out_scratch = refs.pop(0)

    def joined(which):
        pieces = [ref[which, 0] for ref in kv_refs]
        pieces = [piece.reshape(-1, piece.shape[-1]) for piece in pieces]
        return pieces[0] if len(pieces) == 1 else jnp.concatenate(pieces, axis=0)

    keys = joined(0)
    values = joined(1)
    values = jnp.concatenate([values, jnp.ones_like(values)], axis=1)
    factor = score_scale * LOG2E
    slots, inner = q_ref.shape[1], q_ref.shape[2]
    queries = q_ref[0].reshape(slots * inner, q_ref.shape[3])
    for first, count, bias_row in tiles:
        scores = lax.dot_general(
            queries[first : first + count],
            keys,
            (((1,), (1,)), ((), ())),
            preferred_element_type=jnp.float32,
        )
        if has_bias:
            scores = scores * factor + bias_ref[bias_row : bias_row + 1, :]
            peak = jnp.max(scores, axis=1, keepdims=True)
            if has_state:
                peak = jnp.maximum(peak, state_in[0][0, first : first + count, :1])
            weights = jnp.exp2(scores - peak)
        else:
            peak = jnp.max(scores, axis=1, keepdims=True)
            weights = jnp.exp2(scores * factor - peak * factor)
        mixed = jnp.dot(weights.astype(jnp.bfloat16), values, preferred_element_type=jnp.float32)
        value_sum = mixed[:, :128]
        total = mixed[:, 128:]
        if has_state:
            keep = jnp.exp2(state_in[0][0, first : first + count, :] - peak)
            value_sum = value_sum + keep * state_in[2][0, first : first + count, :]
            total = total + keep * state_in[1][0, first : first + count, :]
        if first < state_rows:
            state_out[0][0, first : first + count, :] = jnp.broadcast_to(peak, (count, 128))
            state_out[1][0, first : first + count, :] = total
            state_out[2][0, first : first + count, :] = value_sum
        else:
            low = first - state_rows
            out_scratch[low : low + count, :] = value_sum / total
    share = inner // owners
    me = own_x[0]
    done = out_scratch.shape[0] // inner
    for slot in range(done):
        base = slot * inner
        mine_start = pl.multiple_of(base + me * share, ROW_TILE)
        mine_ref[0, slot] = out_scratch[pl.ds(mine_start, share), :].astype(jnp.bfloat16)
        their_start = pl.multiple_of(base + (owners - 1 - me) * share, ROW_TILE)
        theirs_ref[0, slot] = out_scratch[pl.ds(their_start, share), :].astype(jnp.bfloat16)


def attention(own_x, queries, first_slot, parts, bias, state, state_rows, tiles, score_scale, name):
    groups, all_slots, inner, width = queries.shape
    slots = sum(count for _, count, _ in tiles) // inner
    owners = 2
    done = slots - state_rows // inner
    in_specs = [
        pl.BlockSpec((1, slots, inner, width), lambda h, x: (h, first_slot // slots, 0, 0))
    ]
    operands = [queries]
    for part in parts:
        in_specs.append(
            pl.BlockSpec((2, 1) + part.shape[2:], lambda h, x: (0, h, 0, 0, 0))
        )
        operands.append(part)
    key_count = sum(part.shape[2] * part.shape[3] for part in parts)
    if bias is not None:
        in_specs.append(pl.BlockSpec(bias.shape, lambda h, x: (0, 0)))
        operands.append(bias)
    if state is not None:
        for item in state:
            in_specs.append(pl.BlockSpec((1,) + item.shape[1:], lambda h, x: (h, 0, 0)))
            operands.append(item)
    share = inner // owners
    out_shape = [jax.ShapeDtypeStruct((groups, done, share, width), jnp.bfloat16)] * 2
    out_specs = [pl.BlockSpec((1, done, share, width), lambda h, x: (h, 0, 0, 0))] * 2
    if state_rows:
        out_shape += [jax.ShapeDtypeStruct((groups, state_rows, width), jnp.float32)] * 3
        out_specs += [pl.BlockSpec((1, state_rows, width), lambda h, x: (h, 0, 0))] * 3
    rows = slots * inner
    return pl.pallas_call(
        functools.partial(
            attention_kernel,
            parts=len(parts),
            tiles=tiles,
            has_bias=bias is not None,
            has_state=state is not None,
            state_rows=state_rows,
            owners=owners,
            score_scale=score_scale,
        ),
        out_shape=out_shape,
        grid_spec=pltpu.PrefetchScalarGridSpec(
            num_scalar_prefetch=1,
            grid=(groups,),
            in_specs=in_specs,
            out_specs=out_specs,
            scratch_shapes=[pltpu.VMEM((done * inner, width), jnp.float32)],
        ),
        compiler_params=pltpu.CompilerParams(vmem_limit_bytes=56 << 20),
        cost_estimate=pl.CostEstimate(
            flops=12 * groups * rows * key_count * width,
            transcendentals=groups * rows * key_count,
            bytes_accessed=4 * groups * width * (rows + key_count),
        ),
        name=name,
    )(own_x, *operands)


def project_kernel(table, own_core, *refs, slots, class_slots, groups, inner):
    count = len(class_slots)
    sources = [refs[:count], refs[count : 2 * count]]
    own_weight, same_half, other_half, out_ref, by_slot, by_residue, moved = refs[2 * count :]
    block = pl.program_id(0)
    size = slots * ROW_TILE
    half = groups // 2
    for source in range(2):
        for head in range(groups):
            start = 0
            for ref, taken in zip(sources[source], class_slots):
                by_slot[head, start : start + taken] = ref[head]
                start += taken
            for residue in range(slots):
                slot = table[source * groups + head, residue]
                by_residue[source * 2 + head // half, residue, :, (head % half) * 128 : (head % half + 1) * 128] = by_slot[head, slot]
    core = own_core[0]

    def rows_of(index):
        return by_residue[index].reshape(size, half * 128)

    depth = half * 128
    result = jnp.dot(rows_of(0), own_weight[:depth], preferred_element_type=jnp.float32)
    result += jnp.dot(rows_of(1), own_weight[depth:], preferred_element_type=jnp.float32)
    result += jnp.dot(rows_of(2 + core), same_half[...], preferred_element_type=jnp.float32)
    result += jnp.dot(rows_of(3 - core), other_half[...], preferred_element_type=jnp.float32)
    moved[...] = result.astype(jnp.bfloat16)
    order = one_hot_order(size, slots, True)
    out_ref[...] = jnp.dot(order, moved[...], preferred_element_type=jnp.float32).astype(
        jnp.bfloat16
    )


def project(table, own_core, mine, received, own_weight, same_half, other_half, slots):
    groups, _, share, width = mine[0].shape
    rows = slots * share
    size = slots * ROW_TILE
    blocks = rows // size
    cols = own_weight.shape[1]
    class_slots = [item.shape[1] for item in mine]
    attended_specs = [
        pl.BlockSpec((groups, taken, ROW_TILE, width), lambda b, t, c: (0, 0, b, 0))
        for taken in class_slots
    ]
    whole = lambda b, t, c: (0, 0)
    return pl.pallas_call(
        functools.partial(
            project_kernel, slots=slots, class_slots=class_slots, groups=groups, inner=share
        ),
        out_shape=jax.ShapeDtypeStruct((rows, cols), jnp.bfloat16),
        grid_spec=pltpu.PrefetchScalarGridSpec(
            num_scalar_prefetch=2,
            grid=(blocks,),
            in_specs=attended_specs
            + attended_specs
            + [
                pl.BlockSpec(own_weight.shape, whole, pipeline_mode=pl.Buffered(1)),
                pl.BlockSpec(same_half.shape, whole, pipeline_mode=pl.Buffered(1)),
                pl.BlockSpec(other_half.shape, whole, pipeline_mode=pl.Buffered(1)),
            ],
            out_specs=pl.BlockSpec((size, cols), lambda b, t, c: (b, 0)),
            scratch_shapes=[
                pltpu.VMEM((groups, slots, ROW_TILE, width), jnp.bfloat16),
                pltpu.VMEM((4, slots, ROW_TILE, groups // 2 * width), jnp.bfloat16),
                pltpu.VMEM((size, cols), jnp.bfloat16),
            ],
        ),
        compiler_params=pltpu.CompilerParams(vmem_limit_bytes=56 << 20),
        cost_estimate=pl.CostEstimate(
            flops=2 * rows * 2 * groups * width * cols,
            transcendentals=0,
            bytes_accessed=2 * (4 * groups * width * cols // 2 + rows * cols + rows * 2 * groups * width),
        ),
        name="project",
    )(table, own_core, *mine, *received, own_weight, same_half, other_half)


def bias_rows(query_classes, parts, levels, inner):
    rows = []
    for query_class in query_classes:
        row = []
        for low, high, distance in parts:
            for slot in range(low, high):
                shared = min(query_class, slot_class(slot, levels)) - distance + 1
                row += [math.log2(shared) if shared > 0 else MASKED] * inner
        rows.append(row)
    return jnp.asarray(np.array(rows, np.float32))


def fast_body(query_rows, key_rows, value_rows, head_phase, out_weight):
    shards = lax.axis_size("seq")
    levels = shards.bit_length() - 1
    groups = head_phase.shape[0]
    rows = query_rows.shape[0]
    inner = rows // shards
    slots = shards
    score_scale = 1.0 / math.sqrt(query_rows.shape[1] // groups)
    own_x = lax.axis_index("head").reshape(1)
    own_core = (lax.axis_index("seq") % 2).reshape(1)
    reversed_bits = jnp.asarray([bit_reverse(slot, levels) for slot in range(slots)], jnp.int32)
    phase = head_phase % shards
    residue_table = reversed_bits[None, :] ^ phase[:, None]
    other_phase = swapped(phase, "head", 0)

    half_rows = out_weight.shape[0] // 2
    half_weight = lax.dynamic_slice_in_dim(out_weight, own_core[0] * half_rows, half_rows, 0)
    cuts = [(slots // 2, slots)] + [(0, slots >> level) for level in range(1, levels + 1)]
    ordered = reorder(residue_table, [key_rows, value_rows], slots, cuts)
    first_class, prefixes = ordered[0], ordered[1:]
    same_half = swapped(half_weight, "head", 0)
    queries = reorder(residue_table, [query_rows], slots, [(0, slots)])[0][0]

    remote = []
    for level in range(1, levels + 1):
        pieces = [swapped(prefixes[level - 1], "seq", level - 1)]
        for bit in range(level - 2, -1, -1):
            pieces = pieces + [swapped(piece, "seq", bit) for piece in pieces]
        remote.append(pieces)
    other_half = swapped(same_half, "seq", 0)

    own = [prefixes[0], first_class]
    own_parts = [(0, slots, 0)]

    def remote_parts(level):
        return [(0, slots >> level, level)] * (2 ** (level - 1))

    mine, theirs = [], []
    count = slots // 2 * inner
    tile = 256
    tiles = [(first, tile, 0) for first in range(0, count, tile)]
    out = attention(own_x, queries, slots // 2, own, None, None, 0, tiles, score_scale, "class0")
    mine.append(out[0])
    theirs.append(out[1])
    count = slots // 4 * inner
    tile = 192
    bias = bias_rows([1], own_parts + remote_parts(1), levels, inner)
    tiles = [(first, tile, 0) for first in range(0, count, tile)]
    out = attention(
        own_x, queries, slots // 4, own + remote[0], bias, None, 0, tiles, score_scale, "class1"
    )
    mine.append(out[0])
    theirs.append(out[1])
    late = 2 * inner
    tiles = [(0, inner, 0), (inner, inner, 1), (2 * inner, 2 * inner, 2)]
    bias = bias_rows(
        [levels, levels - 1, levels - 2],
        own_parts + remote_parts(1) + remote_parts(2),
        levels,
        inner,
    )
    out = attention(
        own_x,
        queries,
        0,
        own + remote[0] + remote[1],
        bias,
        None,
        late,
        tiles,
        score_scale,
        "class2",
    )
    mine.append(out[0])
    theirs.append(out[1])
    state = out[2:]
    tiles = [(0, inner, 0), (inner, inner, 1)]
    bias = bias_rows([levels, levels - 1], remote_parts(3) + remote_parts(4), levels, inner)
    out = attention(
        own_x, queries, 0, remote[2] + remote[3], bias, state, 0, tiles, score_scale, "class3"
    )
    mine.append(out[0])
    theirs.append(out[1])

    received = [swapped(item, "head", 0) for item in theirs]
    phases = jnp.concatenate([phase, other_phase])
    inverse = reversed_bits
    slot_table = inverse[jnp.arange(slots, dtype=jnp.int32)[None, :] ^ phases[:, None]]
    return project(
        slot_table,
        own_core,
        mine[::-1],
        received[::-1],
        out_weight,
        same_half,
        other_half,
        slots,
    )


def halve(block, parity, axis):
    shape = block.shape
    shaped = block.reshape(shape[:axis] + (shape[axis] // 2, 2) + shape[axis + 1 :])
    even = lax.index_in_dim(shaped, 0, axis + 1, keepdims=False)
    odd = lax.index_in_dim(shaped, 1, axis + 1, keepdims=False)
    chooser = parity.reshape((-1,) + (1,) * (even.ndim - 1))
    return jnp.where(chooser == 0, even, odd)


def restore(block, fresh, parity, axis):
    shape = block.shape
    shaped = block.reshape(shape[:axis] + (shape[axis] // 2, 2) + shape[axis + 1 :])
    slots = lax.broadcasted_iota(jnp.int32, shaped.shape, axis + 1)
    chooser = parity.reshape((-1,) + (1,) * (shaped.ndim - 1))
    return jnp.where(slots == chooser, jnp.expand_dims(fresh, axis + 1), shaped).reshape(shape)


def attend(queries, key_values, score_scale):

    def score_tile(query_block):
        scores = (
            jnp.einsum(
                "gqd,gkd->gqk", query_block, key_values[:, 0], preferred_element_type=jnp.float32
            )
            * score_scale
        )
        row_peak = jnp.max(scores, axis=2)
        weights = jnp.exp(scores - row_peak[:, :, None])
        row_total = jnp.sum(weights, axis=2)
        row_mixed = jnp.einsum(
            "gqk,gkd->gqd",
            weights.astype(jnp.bfloat16),
            key_values[:, 1],
            preferred_element_type=jnp.float32,
        )
        return (row_peak, row_total, row_mixed)

    query_count = queries.shape[1]
    if query_count > 512 and query_count % 512 == 0:
        results = [
            score_tile(queries[:, first : first + 512]) for first in range(0, query_count, 512)
        ]
        return (
            jnp.concatenate([item[0] for item in results], axis=1),
            jnp.concatenate([item[1] for item in results], axis=1),
            jnp.concatenate([item[2] for item in results], axis=1),
        )
    return score_tile(queries)


def any_body(query_rows, key_rows, value_rows, head_phase, out_weight):
    groups = head_phase.shape[0]
    head_width = query_rows.shape[1] // groups
    levels = lax.axis_size("seq").bit_length() - 1
    score_scale = 1.0 / math.sqrt(head_width)
    bits = [head_phase // 2**level_index % 2 for level_index in range(levels + 1)]

    def head_cols(block, group_index):
        return block[:, group_index * head_width : (group_index + 1) * head_width]

    query_levels = [
        jnp.stack([head_cols(query_rows, group_index) for group_index in range(groups)])
    ]
    own_levels = [
        jnp.stack(
            [
                jnp.stack([head_cols(key_rows, group_index), head_cols(value_rows, group_index)])
                for group_index in range(groups)
            ]
        )
    ]
    for level_index in range(1, levels + 1):
        query_levels.append(halve(query_levels[-1], bits[level_index - 1], 1))
        own_levels.append(halve(own_levels[-1], bits[level_index - 1], 2))
    key_values = {0: own_levels[0]}
    for level_index in range(1, levels + 1):
        block_rows = own_levels[level_index]
        for bit_index in range(level_index):
            block_rows = jnp.concatenate(
                (block_rows, swapped(block_rows, "seq", bit_index)), axis=2
            )
        key_values[level_index] = block_rows
    outcomes = [
        attend(query_levels[level_index], key_values[level_index], score_scale)
        for level_index in range(levels + 1)
    ]
    peak_now, total_now, sum_now = outcomes[levels]
    for level_index in range(levels - 1, -1, -1):
        level_peak, level_total, level_sum = outcomes[level_index]
        parity = bits[level_index]
        old_peak = halve(level_peak, parity, 1)
        old_total = halve(level_total, parity, 1)
        old_sum = halve(level_sum, parity, 1)
        new_peak = jnp.maximum(old_peak, peak_now)
        keep_scale = jnp.exp(old_peak - new_peak)
        fresh_scale = jnp.exp(peak_now - new_peak)
        new_total = old_total * keep_scale + total_now * fresh_scale
        new_sum = old_sum * keep_scale[:, :, None] + sum_now * fresh_scale[:, :, None]
        peak_now = restore(level_peak, new_peak, parity, 1)
        total_now = restore(level_total, new_total, parity, 1)
        sum_now = restore(level_sum, new_sum, parity, 1)
    normed = (sum_now / total_now[:, :, None]).astype(jnp.bfloat16)
    attended = jnp.concatenate([normed[group_index] for group_index in range(groups)], axis=1)
    return lax.psum_scatter(
        jnp.dot(attended, out_weight, preferred_element_type=jnp.float32).astype(jnp.bfloat16),
        "head",
        scatter_dimension=0,
        tiled=True,
    )


def solution(mesh):
    in_specs = (P("seq", "head"), P("seq", "head"), P("seq", "head"), P("head"), P("head", None))
    out_specs = P(("seq", "head"), None)

    def body(query_rows, *others):
        shards = mesh.shape["seq"]
        inner = query_rows.shape[0] // shards
        if shards == 16 and mesh.shape["head"] == 2 and inner % (2 * ROW_TILE) == 0:
            return fast_body(query_rows, *others)
        return any_body(query_rows, *others)

    return jax.shard_map(body, mesh=mesh, in_specs=in_specs, out_specs=out_specs, check_vma=False)
```

```python
import functools
import math

import numpy as np
import jax
import jax.numpy as jnp
from jax import lax
from jax.experimental import pallas as pl
from jax.experimental.pallas import tpu as pltpu
from jax.sharding import PartitionSpec as P

ROW_TILE = 16
LOG2E = 1.4426950408889634
MASKED = -1.0e30


def bit_reverse(value, bits):
    result = 0
    for bit in range(bits):
        result |= ((value >> bit) & 1) << (bits - 1 - bit)
    return result


def slot_class(slot, levels):
    return levels - slot.bit_length()


def swapped(value, axis, bit):
    mask = 2**bit
    pairs = [(source, source ^ mask) for source in range(lax.axis_size(axis))]
    return lax.ppermute(value, axis, pairs)


def one_hot_order(size, stride, transposed):
    rows = lax.broadcasted_iota(jnp.int32, (size, size), 0)
    cols = lax.broadcasted_iota(jnp.int32, (size, size), 1)
    if transposed:
        rows, cols = cols, rows
    inner = size // stride
    match = (rows % inner) * stride + rows // inner == cols
    return jnp.where(match, 1.0, 0.0).astype(jnp.bfloat16)


def reorder_kernel(table, *refs, sources, groups, slots, cuts):
    source_refs = refs[:sources]
    out_refs = refs[sources:-1]
    orders = refs[-1]
    size = slots * ROW_TILE

    @pl.when(pl.program_id(0) == 0)
    def _():
        cols = lax.broadcasted_iota(jnp.int32, (ROW_TILE, size), 1)
        offset = cols - slots * lax.broadcasted_iota(jnp.int32, (ROW_TILE, size), 0)
        for head in range(groups):
            for slot in range(slots):
                match = jnp.where(offset == table[head, slot], 1.0, 0.0)
                orders[head, slot * ROW_TILE : (slot + 1) * ROW_TILE] = match.astype(jnp.bfloat16)

    for head in range(groups):
        pieces = [ref[:, head * 128 : (head + 1) * 128] for ref in source_refs]
        block = pieces[0] if sources == 1 else jnp.concatenate(pieces, axis=1)
        moved = jnp.dot(orders[head], block, preferred_element_type=jnp.float32)
        moved = moved.astype(jnp.bfloat16)
        for index in range(sources):
            piece = moved[:, index * 128 : (index + 1) * 128].reshape(slots, ROW_TILE, 128)
            for out_ref, (low, high) in zip(out_refs, cuts):
                out_ref[index, head] = piece[low:high]


def reorder(table, arrays, slots, cuts, name):
    rows, cols = arrays[0].shape
    groups = cols // 128
    size = slots * ROW_TILE
    blocks = rows // size
    inner = rows // slots
    sources = len(arrays)
    out_shape = [
        jax.ShapeDtypeStruct((sources, groups, high - low, inner, 128), jnp.bfloat16)
        for low, high in cuts
    ]
    total = sum(high - low for low, high in cuts)
    return pl.pallas_call(
        functools.partial(
            reorder_kernel, sources=sources, groups=groups, slots=slots, cuts=cuts
        ),
        out_shape=out_shape,
        grid_spec=pltpu.PrefetchScalarGridSpec(
            num_scalar_prefetch=1,
            grid=(blocks,),
            in_specs=[pl.BlockSpec((size, cols), lambda b, t: (b, 0))] * sources,
            out_specs=[
                pl.BlockSpec(
                    (sources, groups, high - low, ROW_TILE, 128), lambda b, t: (0, 0, 0, b, 0)
                )
                for low, high in cuts
            ],
            scratch_shapes=[pltpu.VMEM((groups, size, size), jnp.bfloat16)],
        ),
        compiler_params=pltpu.CompilerParams(vmem_limit_bytes=56 << 20),
        cost_estimate=pl.CostEstimate(
            flops=2 * sources * rows * size * cols,
            transcendentals=0,
            bytes_accessed=2 * sources * rows * cols + 2 * sources * groups * total * inner * 128,
        ),
        name=name,
    )(table, *arrays)


def attention_kernel(
    own_x, q_ref, *refs, heads, parts, tiles, has_bias, has_state, state_rows, owners, score_scale
):
    refs = list(refs)
    kv_refs = [refs.pop(0) for _ in range(parts)]
    bias_ref = refs.pop(0) if has_bias else None
    state_in = [refs.pop(0) for _ in range(3)] if has_state else None
    mine_ref = refs.pop(0)
    theirs_ref = refs.pop(0)
    state_out = [refs.pop(0) for _ in range(3)] if state_rows else None
    out_scratch = refs.pop(0)
    factor = score_scale * LOG2E
    slots, inner, width = q_ref.shape[1:]

    def joined(which, head):
        pieces = [ref[which, head].reshape(-1, width) for ref in kv_refs]
        return pieces[0] if len(pieces) == 1 else jnp.concatenate(pieces, axis=0)

    def score(unit):
        head, (first, count, _) = unit
        queries = q_ref[head].reshape(slots * inner, width)[first : first + count]
        return lax.dot_general(
            queries, joined(0, head), (((1,), (1,)), ((), ())), preferred_element_type=jnp.float32
        )

    def finish(unit, scores):
        head, (first, count, subs) = unit
        weights, peaks = [], []
        row = 0
        for sub_count, bias_row in subs:
            block = scores[row : row + sub_count]
            if has_bias:
                block = block * factor + bias_ref[bias_row : bias_row + 1, :]
                peak = jnp.max(block, axis=1, keepdims=True)
                if has_state:
                    low = first + row
                    peak = jnp.maximum(peak, state_in[0][head, low : low + sub_count, :1])
                weight = jnp.exp2(block - peak)
            else:
                peak = jnp.max(block, axis=1, keepdims=True)
                weight = jnp.exp2(block * factor - peak * factor)
            weights.append(weight.astype(jnp.bfloat16))
            peaks.append(peak)
            row += sub_count
        weight = weights[0] if len(weights) == 1 else jnp.concatenate(weights, axis=0)
        values = joined(1, head)
        values = jnp.concatenate([values, jnp.ones_like(values)], axis=1)
        mixed = jnp.dot(weight, values, preferred_element_type=jnp.float32)
        value_sum = mixed[:, :width]
        total = mixed[:, width:]
        if has_state or first < state_rows:
            peak = peaks[0] if len(peaks) == 1 else jnp.concatenate(peaks, axis=0)
        if has_state:
            keep = jnp.exp2(state_in[0][head, first : first + count, :] - peak)
            value_sum = value_sum + keep * state_in[2][head, first : first + count, :]
            total = total + keep * state_in[1][head, first : first + count, :]
        if first < state_rows:
            state_out[0][head, first : first + count, :] = jnp.broadcast_to(peak, (count, width))
            state_out[1][head, first : first + count, :] = total
            state_out[2][head, first : first + count, :] = value_sum
        else:
            low = first - state_rows
            out_scratch[head, low : low + count, :] = (value_sum / total).astype(jnp.bfloat16)

    units = [(head, tile) for head in range(heads) for tile in tiles]
    scores = score(units[0])
    for index, unit in enumerate(units):
        following = score(units[index + 1]) if index + 1 < len(units) else None
        finish(unit, scores)
        scores = following

    share = inner // owners
    me = own_x[0]
    for head in range(heads):
        for slot in range(out_scratch.shape[1] // inner):
            base = slot * inner
            start = pl.multiple_of(base + me * share, ROW_TILE)
            mine_ref[head, slot] = out_scratch[head, pl.ds(start, share), :]
            start = pl.multiple_of(base + (owners - 1 - me) * share, ROW_TILE)
            theirs_ref[head, slot] = out_scratch[head, pl.ds(start, share), :]


def attention(
    own_x, queries, first_slot, parts, bias, state, state_rows, tiles, heads, score_scale, name
):
    groups, all_slots, inner, width = queries.shape
    slots = sum(count for _, count, _ in tiles) // inner
    owners = 2
    done = slots - state_rows // inner
    in_specs = [
        pl.BlockSpec((heads, slots, inner, width), lambda h, x: (h, first_slot // slots, 0, 0))
    ]
    operands = [queries]
    for part in parts:
        in_specs.append(
            pl.BlockSpec((2, heads) + part.shape[2:], lambda h, x: (0, h, 0, 0, 0))
        )
        operands.append(part)
    key_count = sum(part.shape[2] * part.shape[3] for part in parts)
    if bias is not None:
        in_specs.append(pl.BlockSpec(bias.shape, lambda h, x: (0, 0)))
        operands.append(bias)
    if state is not None:
        for item in state:
            in_specs.append(pl.BlockSpec((heads,) + item.shape[1:], lambda h, x: (h, 0, 0)))
            operands.append(item)
    share = inner // owners
    out_shape = [jax.ShapeDtypeStruct((groups, done, share, width), jnp.bfloat16)] * 2
    out_specs = [pl.BlockSpec((heads, done, share, width), lambda h, x: (h, 0, 0, 0))] * 2
    if state_rows:
        out_shape += [jax.ShapeDtypeStruct((groups, state_rows, width), jnp.float32)] * 3
        out_specs += [pl.BlockSpec((heads, state_rows, width), lambda h, x: (h, 0, 0))] * 3
    rows = slots * inner
    return pl.pallas_call(
        functools.partial(
            attention_kernel,
            heads=heads,
            parts=len(parts),
            tiles=tiles,
            has_bias=bias is not None,
            has_state=state is not None,
            state_rows=state_rows,
            owners=owners,
            score_scale=score_scale,
        ),
        out_shape=out_shape,
        grid_spec=pltpu.PrefetchScalarGridSpec(
            num_scalar_prefetch=1,
            grid=(groups // heads,),
            in_specs=in_specs,
            out_specs=out_specs,
            scratch_shapes=[pltpu.VMEM((heads, done * inner, width), jnp.bfloat16)],
        ),
        compiler_params=pltpu.CompilerParams(vmem_limit_bytes=60 << 20),
        cost_estimate=pl.CostEstimate(
            flops=12 * groups * rows * key_count * width,
            transcendentals=groups * rows * key_count,
            bytes_accessed=groups * rows * key_count,
        ),
        name=name,
    )(own_x, *operands)


def project_kernel(table, halves, *refs, classes, groups, slots, share, last):
    refs = list(refs)
    attended = [refs.pop(0) for _ in classes]
    weights = [refs.pop(0) for _ in range(2)]
    partial_ref = refs.pop(0) if last else None
    out_ref = refs.pop(0)
    by_residue = refs.pop(0)
    half = groups // 2

    @pl.when(pl.program_id(0) == 0)
    def _():
        for head in range(groups):
            slot = 0
            for ref in attended:
                for index in range(ref.shape[1]):
                    start = pl.multiple_of(table[head, slot] * share, ROW_TILE)
                    by_residue[
                        head // half,
                        pl.ds(start, share),
                        (head % half) * 128 : (head % half + 1) * 128,
                    ] = ref[head, index]
                    slot += 1

    result = jnp.dot(by_residue[halves[0]], weights[0][...], preferred_element_type=jnp.float32)
    result += jnp.dot(by_residue[halves[1]], weights[1][...], preferred_element_type=jnp.float32)
    if not last:
        out_ref[...] = result.astype(jnp.bfloat16)
        return
    result = (result + partial_ref[...].astype(jnp.float32)).astype(jnp.bfloat16)
    size = slots * ROW_TILE
    order = one_hot_order(size, slots, True)
    result = result.reshape(slots, share, result.shape[1])
    for block in range(share // ROW_TILE):
        rows = result[:, block * ROW_TILE : (block + 1) * ROW_TILE].reshape(size, -1)
        out_ref[block * size : (block + 1) * size] = jnp.dot(
            order, rows, preferred_element_type=jnp.float32
        ).astype(jnp.bfloat16)


def project(table, halves, attended, weights, partial, name):
    groups, _, share, width = attended[0].shape[-4:]
    classes = [item.shape[-3] for item in attended]
    slots = sum(classes)
    rows = slots * share
    step = 512
    cols = weights[0].shape[-1]
    if len(weights) == 1:
        depth = weights[0].shape[0] // 2
        weights = weights * 2
        in_specs = [pl.BlockSpec(item.shape, lambda n, t, c: (0, 0, 0, 0)) for item in attended]
        for place in (0, 1):
            in_specs.append(pl.BlockSpec((depth, step), lambda n, t, c, place=place: (place, n)))
    else:
        depth = weights[0].shape[0]
        in_specs = [pl.BlockSpec(item.shape, lambda n, t, c: (0, 0, 0, 0)) for item in attended]
        in_specs += [pl.BlockSpec((depth, step), lambda n, t, c: (0, n))] * 2
    operands = list(attended) + list(weights)
    if partial is not None:
        in_specs.append(pl.BlockSpec((rows, step), lambda n, t, c: (0, n)))
        operands.append(partial)
    return pl.pallas_call(
        functools.partial(
            project_kernel,
            classes=classes,
            groups=groups,
            slots=slots,
            share=share,
            last=partial is not None,
        ),
        out_shape=jax.ShapeDtypeStruct((rows, cols), jnp.bfloat16),
        grid_spec=pltpu.PrefetchScalarGridSpec(
            num_scalar_prefetch=2,
            grid=(cols // step,),
            in_specs=in_specs,
            out_specs=pl.BlockSpec((rows, step), lambda n, t, c: (0, n)),
            scratch_shapes=[pltpu.VMEM((2, rows, groups // 2 * width), jnp.bfloat16)],
        ),
        compiler_params=pltpu.CompilerParams(vmem_limit_bytes=56 << 20),
        cost_estimate=pl.CostEstimate(
            flops=2 * rows * groups * width * cols,
            transcendentals=0,
            bytes_accessed=2 * (groups * width * cols + rows * cols + rows * groups * width),
        ),
        name=name,
    )(table, halves, *operands)


def bias_rows(query_classes, parts, levels, inner):
    rows = []
    for query_class in query_classes:
        row = []
        for low, high, distance in parts:
            for slot in range(low, high):
                shared = min(query_class, slot_class(slot, levels)) - distance + 1
                row += [math.log2(shared) if shared > 0 else MASKED] * inner
        rows.append(row)
    return jnp.asarray(np.array(rows, np.float32))


def after(values, *earlier):
    return lax.optimization_barrier((tuple(values), earlier))[0]


def fast_body(query_rows, key_rows, value_rows, head_phase, out_weight):
    shards = lax.axis_size("seq")
    levels = shards.bit_length() - 1
    groups = head_phase.shape[0]
    rows = query_rows.shape[0]
    inner = rows // shards
    slots = shards
    score_scale = 1.0 / math.sqrt(query_rows.shape[1] // groups)
    own_x = lax.axis_index("head").reshape(1)
    own_core = lax.axis_index("seq") % 2
    reversed_bits = jnp.asarray([bit_reverse(slot, levels) for slot in range(slots)], jnp.int32)
    phase = head_phase % shards
    residue_table = reversed_bits[None, :] ^ phase[:, None]
    over = lambda value, mask: lax.ppermute(
        value, "seq", [(source, source ^ mask) for source in range(shards)]
    )
    head_swap = lambda value: swapped(value, "head", 0)

    half_rows = out_weight.shape[0] // 2
    half_weight = lax.dynamic_slice_in_dim(out_weight, own_core * half_rows, half_rows, 0)
    same_half = head_swap(half_weight)

    (value_rows,) = after([value_rows], half_weight)
    cuts = [(slots // 2, slots)] + [(0, slots >> level) for level in range(1, levels + 1)]
    class_0, level_1, level_2, level_3, level_4 = reorder(
        residue_table, [key_rows, value_rows], slots, cuts, "reorder_kv"
    )
    y_level_2 = over(level_2, 2)
    z_level_3 = over(level_3, 4)
    core_level_1 = over(level_1, 1)
    w_level_4 = over(level_4, 8)
    (query_rows,) = after([query_rows], class_0)
    queries = reorder(residue_table, [query_rows], slots, [(0, slots)], "reorder_q")[0][0]
    (core_level_1,) = after([core_level_1], queries)
    queries, sent_level_4 = after([queries, level_4], core_level_1)
    zw_level_4 = over(sent_level_4, 12)

    own = [level_1, class_0]
    own_parts = [(0, slots, 0)]
    near = own + [core_level_1]
    near_parts = own_parts + [(0, slots // 2, 1)]

    def plain(total, tile, bias_row):
        return [(first, tile, [(tile, bias_row)]) for first in range(0, total, tile)]

    attend = functools.partial(attention, own_x, queries)
    tiles = plain(slots // 2 * inner, 256, 0)
    mine_0, theirs_0 = attend(slots // 2, own, None, None, 0, tiles, 2, score_scale, "class0")
    z_level_3, core_level_1 = after([z_level_3, core_level_1], mine_0)
    near[-1] = core_level_1
    cz_level_3 = over(z_level_3, 1)
    bias = bias_rows([1], near_parts, levels, inner)
    tiles = plain(slots // 4 * inner, 192, 0)
    mine_1, theirs_1 = attend(slots // 4, near, bias, None, 0, tiles, 2, score_scale, "class1")
    y_level_2, w_level_4, zw_level_4, cz_level_3, same_half, theirs_0 = after(
        [y_level_2, w_level_4, zw_level_4, cz_level_3, same_half, theirs_0], mine_1
    )
    cy_level_2 = over(y_level_2, 1)
    got_0 = head_swap(theirs_0)
    yz_level_3 = over(y_level_2[:, :, :2], 4)
    own_level_4 = jnp.concatenate([w_level_4, zw_level_4], axis=2)
    y_level_4 = over(own_level_4, 2)
    got_1 = head_swap(theirs_1)
    late = 2 * inner
    tiles = [
        (0, late, [(inner, 0), (inner, 1)]),
        (late, late, [(late, 2)]),
    ]
    parts = near_parts + [(0, 4, 2)] * 2
    bias = bias_rows([levels, levels - 1, levels - 2], parts, levels, inner)
    mid = [y_level_2, cy_level_2]
    out = attend(0, near + mid, bias, None, late, tiles, 2, score_scale, "class2")
    mine_2, theirs_2 = out[:2]
    state = out[2:]
    yz_level_3, y_level_4, own_level_4, same_half, got_0 = after(
        [yz_level_3, y_level_4, own_level_4, same_half, got_0], mine_2
    )
    cyz_level_3 = over(yz_level_3, 1)
    c_level_4 = over(own_level_4, 1)
    cy_level_4 = over(y_level_4, 1)
    got_2 = head_swap(theirs_2)
    (sent_phase,) = after([phase], mine_2)
    other_phase = head_swap(sent_phase)
    tiles = [(0, late, [(inner, 0), (inner, 1)])]
    parts = [(0, 2, 3)] * 4 + [(0, 1, 4)] * 8
    bias = bias_rows([levels, levels - 1], parts, levels, inner)
    far = [z_level_3, cz_level_3, yz_level_3, cyz_level_3]
    far += [own_level_4, c_level_4, y_level_4, cy_level_4]
    mine_3, theirs_3 = attend(0, far, bias, state, 0, tiles, 4, score_scale, "class3")
    got_3 = head_swap(theirs_3)
    (same_half, got_1, got_2, other_phase) = after([same_half, got_1, got_2, other_phase], mine_3)
    other_half = over(same_half, 1)
    other_table = reversed_bits[None, :] ^ other_phase[:, None]

    partial = project(
        residue_table,
        jnp.asarray([0, 1], jnp.int32),
        [mine_3, mine_2, mine_1, mine_0],
        [out_weight],
        None,
        "project_own",
    )
    (got_3,) = after([got_3], partial)
    halves = jnp.stack([own_core, 1 - own_core])
    return project(
        other_table, halves, [got_3, got_2, got_1, got_0], [same_half, other_half], partial, "project"
    )


def halve(block, parity, axis):
    shape = block.shape
    shaped = block.reshape(shape[:axis] + (shape[axis] // 2, 2) + shape[axis + 1 :])
    even = lax.index_in_dim(shaped, 0, axis + 1, keepdims=False)
    odd = lax.index_in_dim(shaped, 1, axis + 1, keepdims=False)
    chooser = parity.reshape((-1,) + (1,) * (even.ndim - 1))
    return jnp.where(chooser == 0, even, odd)


def restore(block, fresh, parity, axis):
    shape = block.shape
    shaped = block.reshape(shape[:axis] + (shape[axis] // 2, 2) + shape[axis + 1 :])
    slots = lax.broadcasted_iota(jnp.int32, shaped.shape, axis + 1)
    chooser = parity.reshape((-1,) + (1,) * (shaped.ndim - 1))
    return jnp.where(slots == chooser, jnp.expand_dims(fresh, axis + 1), shaped).reshape(shape)


def attend(queries, key_values, score_scale):

    def score_tile(query_block):
        scores = (
            jnp.einsum(
                "gqd,gkd->gqk", query_block, key_values[:, 0], preferred_element_type=jnp.float32
            )
            * score_scale
        )
        row_peak = jnp.max(scores, axis=2)
        weights = jnp.exp(scores - row_peak[:, :, None])
        row_total = jnp.sum(weights, axis=2)
        row_mixed = jnp.einsum(
            "gqk,gkd->gqd",
            weights.astype(jnp.bfloat16),
            key_values[:, 1],
            preferred_element_type=jnp.float32,
        )
        return (row_peak, row_total, row_mixed)

    query_count = queries.shape[1]
    if query_count > 512 and query_count % 512 == 0:
        results = [
            score_tile(queries[:, first : first + 512]) for first in range(0, query_count, 512)
        ]
        return (
            jnp.concatenate([item[0] for item in results], axis=1),
            jnp.concatenate([item[1] for item in results], axis=1),
            jnp.concatenate([item[2] for item in results], axis=1),
        )
    return score_tile(queries)


def any_body(query_rows, key_rows, value_rows, head_phase, out_weight):
    groups = head_phase.shape[0]
    head_width = query_rows.shape[1] // groups
    levels = lax.axis_size("seq").bit_length() - 1
    score_scale = 1.0 / math.sqrt(head_width)
    bits = [head_phase // 2**level_index % 2 for level_index in range(levels + 1)]

    def head_cols(block, group_index):
        return block[:, group_index * head_width : (group_index + 1) * head_width]

    query_levels = [
        jnp.stack([head_cols(query_rows, group_index) for group_index in range(groups)])
    ]
    own_levels = [
        jnp.stack(
            [
                jnp.stack([head_cols(key_rows, group_index), head_cols(value_rows, group_index)])
                for group_index in range(groups)
            ]
        )
    ]
    for level_index in range(1, levels + 1):
        query_levels.append(halve(query_levels[-1], bits[level_index - 1], 1))
        own_levels.append(halve(own_levels[-1], bits[level_index - 1], 2))
    key_values = {0: own_levels[0]}
    for level_index in range(1, levels + 1):
        block_rows = own_levels[level_index]
        for bit_index in range(level_index):
            block_rows = jnp.concatenate(
                (block_rows, swapped(block_rows, "seq", bit_index)), axis=2
            )
        key_values[level_index] = block_rows
    outcomes = [
        attend(query_levels[level_index], key_values[level_index], score_scale)
        for level_index in range(levels + 1)
    ]
    peak_now, total_now, sum_now = outcomes[levels]
    for level_index in range(levels - 1, -1, -1):
        level_peak, level_total, level_sum = outcomes[level_index]
        parity = bits[level_index]
        old_peak = halve(level_peak, parity, 1)
        old_total = halve(level_total, parity, 1)
        old_sum = halve(level_sum, parity, 1)
        new_peak = jnp.maximum(old_peak, peak_now)
        keep_scale = jnp.exp(old_peak - new_peak)
        fresh_scale = jnp.exp(peak_now - new_peak)
        new_total = old_total * keep_scale + total_now * fresh_scale
        new_sum = old_sum * keep_scale[:, :, None] + sum_now * fresh_scale[:, :, None]
        peak_now = restore(level_peak, new_peak, parity, 1)
        total_now = restore(level_total, new_total, parity, 1)
        sum_now = restore(level_sum, new_sum, parity, 1)
    normed = (sum_now / total_now[:, :, None]).astype(jnp.bfloat16)
    attended = jnp.concatenate([normed[group_index] for group_index in range(groups)], axis=1)
    return lax.psum_scatter(
        jnp.dot(attended, out_weight, preferred_element_type=jnp.float32).astype(jnp.bfloat16),
        "head",
        scatter_dimension=0,
        tiled=True,
    )


def solution(mesh):
    in_specs = (P("seq", "head"), P("seq", "head"), P("seq", "head"), P("head"), P("head", None))
    out_specs = P(("seq", "head"), None)

    def body(query_rows, *others):
        shards = mesh.shape["seq"]
        inner = query_rows.shape[0] // shards
        if shards == 16 and mesh.shape["head"] == 2 and inner % (2 * ROW_TILE) == 0:
            return fast_body(query_rows, *others)
        return any_body(query_rows, *others)

    return jax.shard_map(body, mesh=mesh, in_specs=in_specs, out_specs=out_specs, check_vma=False)
```

```python
import functools
import math

import numpy as np
import jax
import jax.numpy as jnp
from jax import lax
from jax.experimental import pallas as pl
from jax.experimental.pallas import tpu as pltpu
from jax.sharding import PartitionSpec as P

ROW_TILE = 16
LOG2E = 1.4426950408889634
MASKED = -1.0e30


def bit_reverse(value, bits):
    result = 0
    for bit in range(bits):
        result |= ((value >> bit) & 1) << (bits - 1 - bit)
    return result


def slot_class(slot, levels):
    return levels - slot.bit_length()


def swapped(value, axis, bit):
    mask = 2**bit
    pairs = [(source, source ^ mask) for source in range(lax.axis_size(axis))]
    return lax.ppermute(value, axis, pairs)


def one_hot_order(size, stride, transposed):
    rows = lax.broadcasted_iota(jnp.int32, (size, size), 0)
    cols = lax.broadcasted_iota(jnp.int32, (size, size), 1)
    if transposed:
        rows, cols = cols, rows
    inner = size // stride
    match = (rows % inner) * stride + rows // inner == cols
    return jnp.where(match, 1.0, 0.0).astype(jnp.bfloat16)


def slot_order(table, head, slots):
    size = slots * ROW_TILE
    cols = lax.broadcasted_iota(jnp.int32, (ROW_TILE, size), 1)
    offset = cols - slots * lax.broadcasted_iota(jnp.int32, (ROW_TILE, size), 0)
    pieces = [
        jnp.where(offset == table[head, slot], 1.0, 0.0).astype(jnp.bfloat16)
        for slot in range(slots)
    ]
    return jnp.concatenate(pieces, axis=0)


def reorder_kernel(table, key_ref, value_ref, *refs, groups, slots, cuts, blocks):
    count = len(cuts)
    out_refs = refs[:count]
    source, orders = refs[count : count + 2]
    moved_refs = refs[count + 2 : 2 * count + 2]
    in_sems, out_sems = refs[2 * count + 2 :]
    size = slots * ROW_TILE

    def fetch(block, index):
        rows = pl.ds(block * size, size)
        ref = (key_ref, value_ref)[index]
        return pltpu.make_async_copy(
            ref.at[rows], source.at[index, rows], in_sems.at[block, index]
        )

    def send(block, place):
        return pltpu.make_async_copy(
            moved_refs[place].at[block],
            out_refs[place].at[:, :, :, pl.ds(block * ROW_TILE, ROW_TILE)],
            out_sems.at[block, place],
        )

    for block in range(blocks):
        for index in range(2):
            fetch(block, index).start()
    for head in range(groups):
        orders[head] = slot_order(table, head, slots)
    for block in range(blocks):
        for index in range(2):
            fetch(block, index).wait()
        for head in range(groups):
            rows = slice(block * size, (block + 1) * size)
            cols = slice(head * 128, (head + 1) * 128)
            pair = jnp.concatenate([source[0, rows, cols], source[1, rows, cols]], axis=1)
            moved = jnp.dot(orders[head], pair, preferred_element_type=jnp.float32)
            moved = moved.astype(jnp.bfloat16)
            for index in range(2):
                piece = moved[:, index * 128 : (index + 1) * 128].reshape(slots, ROW_TILE, 128)
                for ref, (low, high) in zip(moved_refs, cuts):
                    ref[block, index, head] = piece[low:high]
        for place in range(count):
            send(block, place).start()
    for block in range(blocks):
        for place in range(count):
            send(block, place).wait()


def reorder(table, key_rows, value_rows, slots, cuts, name):
    rows, cols = key_rows.shape
    groups = cols // 128
    size = slots * ROW_TILE
    blocks = rows // size
    inner = rows // slots
    out_shape = [
        jax.ShapeDtypeStruct((2, groups, high - low, inner, 128), jnp.bfloat16)
        for low, high in cuts
    ]
    total = sum(high - low for low, high in cuts)
    any_spec = pl.BlockSpec(memory_space=pl.ANY)
    return pl.pallas_call(
        functools.partial(reorder_kernel, groups=groups, slots=slots, cuts=cuts, blocks=blocks),
        out_shape=out_shape,
        grid_spec=pltpu.PrefetchScalarGridSpec(
            num_scalar_prefetch=1,
            grid=(1,),
            in_specs=[any_spec] * 2,
            out_specs=[any_spec] * len(cuts),
            scratch_shapes=[
                pltpu.VMEM((2, rows, cols), jnp.bfloat16),
                pltpu.VMEM((groups, size, size), jnp.bfloat16),
            ]
            + [
                pltpu.VMEM((blocks, 2, groups, high - low, ROW_TILE, 128), jnp.bfloat16)
                for low, high in cuts
            ]
            + [
                pltpu.SemaphoreType.DMA((blocks, 2)),
                pltpu.SemaphoreType.DMA((blocks, len(cuts))),
            ],
        ),
        compiler_params=pltpu.CompilerParams(vmem_limit_bytes=60 << 20),
        cost_estimate=pl.CostEstimate(
            flops=4 * rows * size * cols,
            transcendentals=0,
            bytes_accessed=4 * rows * cols + 4 * groups * total * inner * 128,
        ),
        name=name,
    )(table, key_rows, value_rows)


def attention_kernel(
    own_x,
    table,
    q_ref,
    *refs,
    heads,
    parts,
    first_row,
    tiles,
    moves_queries,
    has_bias,
    has_state,
    state_rows,
    inner,
    owners,
    score_scale,
):
    refs = list(refs)
    kv_refs = [refs.pop(0) for _ in range(parts)]
    bias_ref = refs.pop(0) if has_bias else None
    state_in = [refs.pop(0) for _ in range(3)] if has_state else None
    mine_ref = refs.pop(0)
    theirs_ref = refs.pop(0)
    state_out = [refs.pop(0) for _ in range(3)] if state_rows else None
    rest_ref = refs.pop(0) if moves_queries else None
    out_scratch = refs.pop(0)
    by_slot = refs.pop(0) if moves_queries else None
    factor = score_scale * LOG2E
    slots = table.shape[1]
    width = 128

    def arrange(head):
        order = slot_order(table, pl.program_id(0) * heads + head, slots)
        size = slots * ROW_TILE
        for block in range(q_ref.shape[0] // size):
            tokens = q_ref[block * size : (block + 1) * size, head * width : (head + 1) * width]
            moved = jnp.dot(order, tokens, preferred_element_type=jnp.float32)
            moved = moved.astype(jnp.bfloat16).reshape(slots, ROW_TILE, width)
            by_slot[head, :, block * ROW_TILE : (block + 1) * ROW_TILE] = moved
        rest_ref[head] = by_slot[head, : slots // 2]

    def joined(which, head):
        pieces = []
        for ref in kv_refs:
            if len(ref.shape) == 5:
                pieces.append(ref[which, head].reshape(-1, width))
            else:
                for index in range(ref.shape[0]):
                    pieces.append(ref[index, which, head].reshape(-1, width))
        return pieces[0] if len(pieces) == 1 else jnp.concatenate(pieces, axis=0)

    def score(unit):
        head, (first, count, _) = unit
        if moves_queries:
            if first == tiles[0][0]:
                arrange(head)
            queries = by_slot[head].reshape(slots * inner, width)
            queries = queries[first_row + first : first_row + first + count]
        else:
            queries = q_ref[head].reshape(-1, width)[first : first + count]
        return lax.dot_general(
            queries, joined(0, head), (((1,), (1,)), ((), ())), preferred_element_type=jnp.float32
        )

    def finish(unit, scores):
        head, (first, count, subs) = unit
        weights, peaks = [], []
        row = 0
        for sub_count, bias_row in subs:
            block = scores[row : row + sub_count]
            if has_bias:
                block = block * factor + bias_ref[bias_row : bias_row + 1, :]
                peak = jnp.max(block, axis=1, keepdims=True)
                if has_state:
                    low = first + row
                    peak = jnp.maximum(peak, state_in[0][head, low : low + sub_count, :1])
                weight = jnp.exp2(block - peak)
            else:
                peak = jnp.max(block, axis=1, keepdims=True)
                weight = jnp.exp2(block * factor - peak * factor)
            weights.append(weight.astype(jnp.bfloat16))
            peaks.append(peak)
            row += sub_count
        weight = weights[0] if len(weights) == 1 else jnp.concatenate(weights, axis=0)
        values = joined(1, head)
        values = jnp.concatenate([values, jnp.ones_like(values)], axis=1)
        mixed = jnp.dot(weight, values, preferred_element_type=jnp.float32)
        value_sum = mixed[:, :width]
        total = mixed[:, width:]
        if has_state or first < state_rows:
            peak = peaks[0] if len(peaks) == 1 else jnp.concatenate(peaks, axis=0)
        if has_state:
            keep = jnp.exp2(state_in[0][head, first : first + count, :] - peak)
            value_sum = value_sum + keep * state_in[2][head, first : first + count, :]
            total = total + keep * state_in[1][head, first : first + count, :]
        if first < state_rows:
            state_out[0][head, first : first + count, :] = jnp.broadcast_to(peak, (count, width))
            state_out[1][head, first : first + count, :] = total
            state_out[2][head, first : first + count, :] = value_sum
        else:
            low = first - state_rows
            out_scratch[head, low : low + count, :] = (value_sum / total).astype(jnp.bfloat16)

    units = [(head, tile) for head in range(heads) for tile in tiles]
    scores = score(units[0])
    for index, unit in enumerate(units):
        following = score(units[index + 1]) if index + 1 < len(units) else None
        finish(unit, scores)
        scores = following

    share = inner // owners
    me = own_x[0]
    for head in range(heads):
        for slot in range(out_scratch.shape[1] // inner):
            base = slot * inner
            start = pl.multiple_of(base + me * share, ROW_TILE)
            mine_ref[head, slot] = out_scratch[head, pl.ds(start, share), :]
            start = pl.multiple_of(base + (owners - 1 - me) * share, ROW_TILE)
            theirs_ref[head, slot] = out_scratch[head, pl.ds(start, share), :]


def attention(
    own_x,
    table,
    queries,
    first_slot,
    parts,
    bias,
    state,
    state_rows,
    tiles,
    heads,
    score_scale,
    name,
):
    moves_queries = queries.ndim == 2
    groups, slots = table.shape
    inner, width = parts[0].shape[-2:]
    owners = 2
    rows = sum(count for _, count, _ in tiles)
    taken = rows // inner
    done = (rows - state_rows) // inner
    if moves_queries:
        in_specs = [pl.BlockSpec((queries.shape[0], heads * width), lambda h, x, t: (0, h))]
    else:
        in_specs = [
            pl.BlockSpec((heads, taken, inner, width), lambda h, x, t: (h, first_slot // taken, 0, 0))
        ]
    operands = [queries] + list(parts)
    for part in parts:
        if part.ndim == 5:
            in_specs.append(
                pl.BlockSpec((2, heads) + part.shape[2:], lambda h, x, t: (0, h, 0, 0, 0))
            )
        else:
            in_specs.append(
                pl.BlockSpec(
                    part.shape[:2] + (heads,) + part.shape[3:], lambda h, x, t: (0, 0, h, 0, 0, 0)
                )
            )
    key_count = sum(part.size // (2 * groups * width) for part in parts)
    if bias is not None:
        in_specs.append(pl.BlockSpec(bias.shape, lambda h, x, t: (0, 0)))
        operands.append(bias)
    if state is not None:
        for item in state:
            in_specs.append(pl.BlockSpec((heads,) + item.shape[1:], lambda h, x, t: (h, 0, 0)))
            operands.append(item)
    share = inner // owners
    out_shape = [jax.ShapeDtypeStruct((groups, done, share, width), jnp.bfloat16)] * 2
    out_specs = [pl.BlockSpec((heads, done, share, width), lambda h, x, t: (h, 0, 0, 0))] * 2
    scratch = [pltpu.VMEM((heads, done * inner, width), jnp.bfloat16)]
    if state_rows:
        out_shape += [jax.ShapeDtypeStruct((groups, state_rows, width), jnp.float32)] * 3
        out_specs += [pl.BlockSpec((heads, state_rows, width), lambda h, x, t: (h, 0, 0))] * 3
    if moves_queries:
        rest = (slots // 2, inner, width)
        out_shape.append(jax.ShapeDtypeStruct((groups,) + rest, jnp.bfloat16))
        out_specs.append(pl.BlockSpec((heads,) + rest, lambda h, x, t: (h, 0, 0, 0)))
        scratch.append(pltpu.VMEM((heads, slots, inner, width), jnp.bfloat16))
    return pl.pallas_call(
        functools.partial(
            attention_kernel,
            heads=heads,
            parts=len(parts),
            first_row=first_slot * inner,
            tiles=tiles,
            moves_queries=moves_queries,
            has_bias=bias is not None,
            has_state=state is not None,
            state_rows=state_rows,
            inner=inner,
            owners=owners,
            score_scale=score_scale,
        ),
        out_shape=out_shape,
        grid_spec=pltpu.PrefetchScalarGridSpec(
            num_scalar_prefetch=2,
            grid=(groups // heads,),
            in_specs=in_specs,
            out_specs=out_specs,
            scratch_shapes=scratch,
        ),
        compiler_params=pltpu.CompilerParams(vmem_limit_bytes=60 << 20),
        cost_estimate=pl.CostEstimate(
            flops=12 * groups * rows * key_count * width,
            transcendentals=groups * rows * key_count,
            bytes_accessed=groups * rows * key_count,
        ),
        name=name,
    )(own_x, table, *operands)


def project_kernel(table, halves, *refs, classes, sources, groups, slots, share, last):
    refs = list(refs)
    attended = [refs.pop(0) for _ in classes]
    weights = [refs.pop(0) for _ in range(sources)]
    partial_ref = refs.pop(0) if last else None
    out_ref = refs.pop(0)
    by_residue = refs.pop(0)
    half = groups // 2

    @pl.when(pl.program_id(0) == 0)
    def _():
        for head in range(groups):
            slot = 0
            for ref in attended:
                for index in range(ref.shape[1]):
                    start = pl.multiple_of(table[head, slot] * share, ROW_TILE)
                    by_residue[
                        halves[head // half],
                        pl.ds(start, share),
                        (head % half) * 128 : (head % half + 1) * 128,
                    ] = ref[head, index]
                    slot += 1

    rows = jnp.concatenate([by_residue[0], by_residue[1]], axis=1)
    weight = jnp.concatenate([ref[...] for ref in weights], axis=0)
    result = jnp.dot(rows, weight, preferred_element_type=jnp.float32)
    if not last:
        out_ref[...] = result.astype(jnp.bfloat16)
        return
    result = (result + partial_ref[...].astype(jnp.float32)).astype(jnp.bfloat16)
    size = slots * ROW_TILE
    order = one_hot_order(size, slots, True)
    result = result.reshape(slots, share, result.shape[1])
    for block in range(share // ROW_TILE):
        rows = result[:, block * ROW_TILE : (block + 1) * ROW_TILE].reshape(size, -1)
        out_ref[block * size : (block + 1) * size] = jnp.dot(
            order, rows, preferred_element_type=jnp.float32
        ).astype(jnp.bfloat16)


def project(table, halves, attended, weights, partial, name):
    groups, _, share, width = attended[0].shape[-4:]
    classes = [item.shape[-3] for item in attended]
    slots = sum(classes)
    rows = slots * share
    step = 512
    cols = weights[0].shape[-1]
    in_specs = [pl.BlockSpec(item.shape, lambda n, t, c: (0, 0, 0, 0)) for item in attended]
    in_specs += [pl.BlockSpec((item.shape[0], step), lambda n, t, c: (0, n)) for item in weights]
    operands = list(attended) + list(weights)
    if partial is not None:
        in_specs.append(pl.BlockSpec((rows, step), lambda n, t, c: (0, n)))
        operands.append(partial)
    return pl.pallas_call(
        functools.partial(
            project_kernel,
            classes=classes,
            sources=len(weights),
            groups=groups,
            slots=slots,
            share=share,
            last=partial is not None,
        ),
        out_shape=jax.ShapeDtypeStruct((rows, cols), jnp.bfloat16),
        grid_spec=pltpu.PrefetchScalarGridSpec(
            num_scalar_prefetch=2,
            grid=(cols // step,),
            in_specs=in_specs,
            out_specs=pl.BlockSpec((rows, step), lambda n, t, c: (0, n)),
            scratch_shapes=[pltpu.VMEM((2, rows, groups // 2 * width), jnp.bfloat16)],
        ),
        compiler_params=pltpu.CompilerParams(vmem_limit_bytes=60 << 20),
        cost_estimate=pl.CostEstimate(
            flops=2 * rows * groups * width * cols,
            transcendentals=0,
            bytes_accessed=2 * (groups * width * cols + rows * cols + rows * groups * width),
        ),
        name=name,
    )(table, halves, *operands)


def bias_rows(query_classes, parts, levels, inner):
    rows = []
    for query_class in query_classes:
        row = []
        for low, high, distance in parts:
            for slot in range(low, high):
                shared = min(query_class, slot_class(slot, levels)) - distance + 1
                row += [math.log2(shared) if shared > 0 else MASKED] * inner
        rows.append(row)
    return jnp.asarray(np.array(rows, np.float32))


def after(values, *earlier):
    return lax.optimization_barrier((tuple(values), earlier))[0]


def fast_body(query_rows, key_rows, value_rows, head_phase, out_weight):
    shards = lax.axis_size("seq")
    levels = shards.bit_length() - 1
    groups = head_phase.shape[0]
    rows = query_rows.shape[0]
    inner = rows // shards
    slots = shards
    score_scale = 1.0 / math.sqrt(query_rows.shape[1] // groups)
    own_x = lax.axis_index("head").reshape(1)
    own_core = lax.axis_index("seq") % 2
    reversed_bits = jnp.asarray([bit_reverse(slot, levels) for slot in range(slots)], jnp.int32)
    phase = head_phase % shards
    residue_table = reversed_bits[None, :] ^ phase[:, None]
    over = lambda value, mask: lax.ppermute(
        value, "seq", [(source, source ^ mask) for source in range(shards)]
    )
    head_swap = lambda value: swapped(value, "head", 0)

    half_rows = out_weight.shape[0] // 2
    half_weight = lax.dynamic_slice_in_dim(out_weight, own_core * half_rows, half_rows, 0)
    same_half = head_swap(half_weight)
    other_phase = head_swap(phase)

    (value_rows,) = after([value_rows], half_weight)
    cuts = [(slots // 2, slots)] + [(0, slots >> level) for level in range(1, levels + 1)]
    class_0, level_1, level_2, level_3, level_4 = reorder(
        residue_table, key_rows, value_rows, slots, cuts, "reorder_kv"
    )
    y_level_2 = over(level_2, 2)
    z_level_3 = over(level_3, 4)
    core_level_1 = over(level_1, 1)
    w_level_4 = over(level_4, 8)
    zw_level_4 = over(level_4, 12)
    query_rows, other_phase = after([query_rows, other_phase], class_0)
    other_table = reversed_bits[None, :] ^ other_phase[:, None]
    query_rows, other_table = after([query_rows], other_table) + (other_table,)

    own = [level_1, class_0]
    own_parts = [(0, slots, 0)]
    near = own + [core_level_1]
    near_parts = own_parts + [(0, slots // 2, 1)]

    def plain(total, tile, bias_row):
        return [(first, tile, [(tile, bias_row)]) for first in range(0, total, tile)]

    attend = functools.partial(attention, own_x, residue_table)
    tiles = plain(slots // 2 * inner, 256, 0)
    mine_0, theirs_0, queries = attend(
        query_rows, slots // 2, own, None, None, 0, tiles, 2, score_scale, "class0"
    )
    z_level_3, core_level_1 = after([z_level_3, core_level_1], mine_0)
    near[-1] = core_level_1
    cz_level_3 = over(z_level_3, 1)
    bias = bias_rows([1], near_parts, levels, inner)
    tiles = plain(slots // 4 * inner, 192, 0)
    mine_1, theirs_1 = attend(
        queries, slots // 4, near, bias, None, 0, tiles, 2, score_scale, "class1"
    )
    y_level_2, w_level_4, zw_level_4, cz_level_3, same_half, theirs_0 = after(
        [y_level_2, w_level_4, zw_level_4, cz_level_3, same_half, theirs_0], mine_1
    )
    cy_level_2 = over(y_level_2, 1)
    got_0 = head_swap(theirs_0)
    yz_level_3 = over(y_level_2[:, :, :2], 4)
    far_level_4 = jnp.stack([w_level_4, zw_level_4])
    y_level_4 = over(far_level_4, 2)
    got_1 = head_swap(theirs_1)
    late = 2 * inner
    tiles = [
        (0, late, [(inner, 0), (inner, 1)]),
        (late, late, [(late, 2)]),
    ]
    parts = near_parts + [(0, 4, 2)] * 2
    bias = bias_rows([levels, levels - 1, levels - 2], parts, levels, inner)
    mid = [y_level_2, cy_level_2]
    out = attend(
        queries, 0, near + mid, bias, None, late, tiles, 2, score_scale, "class2"
    )
    mine_2, theirs_2 = out[:2]
    state = out[2:]
    yz_level_3, y_level_4, far_level_4, same_half, got_0 = after(
        [yz_level_3, y_level_4, far_level_4, same_half, got_0], mine_2
    )
    cyz_level_3 = over(yz_level_3, 1)
    c_level_4 = over(far_level_4, 1)
    cy_level_4 = over(y_level_4, 1)
    got_2 = head_swap(theirs_2)
    tiles = [(0, late, [(inner, 0), (inner, 1)])]
    parts = [(0, 2, 3)] * 4 + [(0, 1, 4)] * 8
    bias = bias_rows([levels, levels - 1], parts, levels, inner)
    far = [z_level_3, cz_level_3, yz_level_3, cyz_level_3]
    far += [far_level_4, c_level_4, y_level_4, cy_level_4]
    mine_3, theirs_3 = attend(
        queries, 0, far, bias, state, 0, tiles, 4, score_scale, "class3"
    )
    got_3 = head_swap(theirs_3)
    (same_half, got_1, got_2) = after([same_half, got_1, got_2], mine_3)
    other_half = over(same_half, 1)

    partial = project(
        residue_table,
        jnp.asarray([0, 1], jnp.int32),
        [mine_3, mine_2, mine_1, mine_0],
        [out_weight],
        None,
        "project_own",
    )
    (got_3,) = after([got_3], partial)
    halves = jnp.stack([own_core, 1 - own_core])
    return project(
        other_table, halves, [got_3, got_2, got_1, got_0], [same_half, other_half], partial, "project"
    )


def halve(block, parity, axis):
    shape = block.shape
    shaped = block.reshape(shape[:axis] + (shape[axis] // 2, 2) + shape[axis + 1 :])
    even = lax.index_in_dim(shaped, 0, axis + 1, keepdims=False)
    odd = lax.index_in_dim(shaped, 1, axis + 1, keepdims=False)
    chooser = parity.reshape((-1,) + (1,) * (even.ndim - 1))
    return jnp.where(chooser == 0, even, odd)


def restore(block, fresh, parity, axis):
    shape = block.shape
    shaped = block.reshape(shape[:axis] + (shape[axis] // 2, 2) + shape[axis + 1 :])
    slots = lax.broadcasted_iota(jnp.int32, shaped.shape, axis + 1)
    chooser = parity.reshape((-1,) + (1,) * (shaped.ndim - 1))
    return jnp.where(slots == chooser, jnp.expand_dims(fresh, axis + 1), shaped).reshape(shape)


def attend(queries, key_values, score_scale):

    def score_tile(query_block):
        scores = (
            jnp.einsum(
                "gqd,gkd->gqk", query_block, key_values[:, 0], preferred_element_type=jnp.float32
            )
            * score_scale
        )
        row_peak = jnp.max(scores, axis=2)
        weights = jnp.exp(scores - row_peak[:, :, None])
        row_total = jnp.sum(weights, axis=2)
        row_mixed = jnp.einsum(
            "gqk,gkd->gqd",
            weights.astype(jnp.bfloat16),
            key_values[:, 1],
            preferred_element_type=jnp.float32,
        )
        return (row_peak, row_total, row_mixed)

    query_count = queries.shape[1]
    if query_count > 512 and query_count % 512 == 0:
        results = [
            score_tile(queries[:, first : first + 512]) for first in range(0, query_count, 512)
        ]
        return (
            jnp.concatenate([item[0] for item in results], axis=1),
            jnp.concatenate([item[1] for item in results], axis=1),
            jnp.concatenate([item[2] for item in results], axis=1),
        )
    return score_tile(queries)


def any_body(query_rows, key_rows, value_rows, head_phase, out_weight):
    groups = head_phase.shape[0]
    head_width = query_rows.shape[1] // groups
    levels = lax.axis_size("seq").bit_length() - 1
    score_scale = 1.0 / math.sqrt(head_width)
    bits = [head_phase // 2**level_index % 2 for level_index in range(levels + 1)]

    def head_cols(block, group_index):
        return block[:, group_index * head_width : (group_index + 1) * head_width]

    query_levels = [
        jnp.stack([head_cols(query_rows, group_index) for group_index in range(groups)])
    ]
    own_levels = [
        jnp.stack(
            [
                jnp.stack([head_cols(key_rows, group_index), head_cols(value_rows, group_index)])
                for group_index in range(groups)
            ]
        )
    ]
    for level_index in range(1, levels + 1):
        query_levels.append(halve(query_levels[-1], bits[level_index - 1], 1))
        own_levels.append(halve(own_levels[-1], bits[level_index - 1], 2))
    key_values = {0: own_levels[0]}
    for level_index in range(1, levels + 1):
        block_rows = own_levels[level_index]
        for bit_index in range(level_index):
            block_rows = jnp.concatenate(
                (block_rows, swapped(block_rows, "seq", bit_index)), axis=2
            )
        key_values[level_index] = block_rows
    outcomes = [
        attend(query_levels[level_index], key_values[level_index], score_scale)
        for level_index in range(levels + 1)
    ]
    peak_now, total_now, sum_now = outcomes[levels]
    for level_index in range(levels - 1, -1, -1):
        level_peak, level_total, level_sum = outcomes[level_index]
        parity = bits[level_index]
        old_peak = halve(level_peak, parity, 1)
        old_total = halve(level_total, parity, 1)
        old_sum = halve(level_sum, parity, 1)
        new_peak = jnp.maximum(old_peak, peak_now)
        keep_scale = jnp.exp(old_peak - new_peak)
        fresh_scale = jnp.exp(peak_now - new_peak)
        new_total = old_total * keep_scale + total_now * fresh_scale
        new_sum = old_sum * keep_scale[:, :, None] + sum_now * fresh_scale[:, :, None]
        peak_now = restore(level_peak, new_peak, parity, 1)
        total_now = restore(level_total, new_total, parity, 1)
        sum_now = restore(level_sum, new_sum, parity, 1)
    normed = (sum_now / total_now[:, :, None]).astype(jnp.bfloat16)
    attended = jnp.concatenate([normed[group_index] for group_index in range(groups)], axis=1)
    return lax.psum_scatter(
        jnp.dot(attended, out_weight, preferred_element_type=jnp.float32).astype(jnp.bfloat16),
        "head",
        scatter_dimension=0,
        tiled=True,
    )


def solution(mesh):
    in_specs = (P("seq", "head"), P("seq", "head"), P("seq", "head"), P("head"), P("head", None))
    out_specs = P(("seq", "head"), None)

    def body(query_rows, *others):
        shards = mesh.shape["seq"]
        inner = query_rows.shape[0] // shards
        if shards == 16 and mesh.shape["head"] == 2 and inner % (2 * ROW_TILE) == 0:
            return fast_body(query_rows, *others)
        return any_body(query_rows, *others)

    return jax.shard_map(body, mesh=mesh, in_specs=in_specs, out_specs=out_specs, check_vma=False)
```
